512 devices in a mesh: kz: 16 (over x, y_hi, core), en: 32 (over y_lo, z).
Axes of the slice: x: 4, y: 4 (y_hi: 2, y_lo: 2; y = y_hi * 2 + y_lo), z: 16, core: 2. Of those that a mesh axis runs over, the one named last changes fastest.
Arguments:
- green: bfloat16 [32, 2, 144, 4096], P('kz', None, None, 'en'), may hold values from -6 to 6
- coupling: bfloat16 [32, 82944], replicated, may hold values from -0.03125 to 0.03125
- kdiff: int32 [32, 32], replicated, may hold values from 0 to 31, each once within a row
- shift: int32 [32], replicated, may hold values from 1 to 8, as said below
- emit_weight: float32 [32], replicated, may hold values from 0.3 to 3
- absorb_weight: float32 [32], replicated, may hold values from 0.3 to 3
- neighbours: int32 [16, 4], replicated, may hold values from 0 to 15
Outputs:
- sigma: float32 [32, 2, 144, 4096], P('kz', None, None, 'en')
The draws below stay inside these ranges and needn't reach their ends.
Inputs may be any that keep to these rules, and one draw needn't show every extreme that they name: `kdiff`: every row names each momentum point once. `shift`: some entry equals 8.
All inputs are finite; a program needn't handle non-finite values.
Results may differ from the reference program's by a relative error of at most 0.0029.
Values may be sent and summed in bfloat16 or wider, within the bound.
A program may use at most 128 MiB of HBM per device.

```python
import math
import jax
import jax.numpy as jnp
from jax import lax

BLK = 144
HALO = 8
NA = 16
NK = 32
NE = 256


def draw_shift(key, part):
    first = jax.random.fold_in(key, 11)
    second = jax.random.fold_in(key, 23)
    values = jax.random.randint(first, (NK,), 1, HALO + 1)
    place = jax.random.randint(second, (), 0, NK)
    return values.at[place].set(HALO).astype(jnp.int32)


def place_ends(result, own_key, least, top_value):
    shape = result.shape
    spot = [jax.random.randint(jax.random.fold_in(own_key, axis), (), 0, shape[axis]) for axis in range(len(shape))]
    result = result.at[tuple(spot)].set(least)
    longest = shape.index(max(shape))
    spot[longest] = (spot[longest] + 1) % shape[longest]
    return result.at[tuple(spot)].set(top_value)


def level_of(key, shape, shards, smallest, high):
    factor_of, own = 1.0, jax.random.fold_in(key, 6)
    for position, parts in shards:
        heights = jnp.exp(jax.random.uniform(jax.random.fold_in(own, position), (parts,), jnp.float32, smallest / len(shards), high / len(shards)))
        factor_of = factor_of * jnp.repeat(heights, shape[position] // parts).reshape([-1 if axis == position else 1 for axis in range(len(shape))])
    return factor_of


def bell_draw(key, dims, scale, bound, split=(), held_as=jnp.bfloat16):
    entries = jax.random.normal(key, dims, jnp.float32) * scale
    if len(split) > 0:
        entries = level_of(key, dims, split, -0.22, 0.18) * entries
    return jnp.clip(entries, min=-bound, max=bound).astype(held_as)


def setup_inputs(seed: int = 0) -> dict:
    seeds = jax.random.split(jax.random.key(seed), 8)
    green = bell_draw(seeds[0], (NK, 2, BLK, NE * NA), 1.0, 6.0, ((0, 16), (3, 32)))
    coupling = bell_draw(seeds[1], (NK, 4 * BLK * BLK), (8 * BLK * NK) ** -0.5, 0.03125)
    kdiff = jax.vmap(lambda own: jax.random.permutation(own, NK))(jax.random.split(seeds[2], NK)).reshape((NK, NK)).astype(jnp.int32)
    shift = draw_shift(jax.random.fold_in(seeds[7], 71), 0)
    emit_weight = jnp.clip(jnp.exp(jax.random.uniform(seeds[4], (NK,), jnp.float32, math.log(0.3), math.log(3.0))), 0.3, 3.0)
    absorb_weight = jnp.clip(jnp.exp(jax.random.uniform(seeds[5], (NK,), jnp.float32, math.log(0.3), math.log(3.0))), 0.3, 3.0)
    neighbours = place_ends(jax.random.randint(seeds[6], (NA, 4), 0, NA), jax.random.fold_in(seeds[6], 1), 0, NA - 1).astype(jnp.int32)
    return {"green": green, "coupling": coupling, "kdiff": kdiff, "shift": shift, "emit_weight": emit_weight, "absorb_weight": absorb_weight, "neighbours": neighbours}


def reference(green, coupling, kdiff, shift, emit_weight, absorb_weight, neighbours):
    cols = NE * NA
    padded = jnp.pad(green, ((0, 0), (0, 0), (0, 0), (HALO * NA, HALO * NA)))
    column = jnp.arange(cols, dtype=jnp.int32)
    index = jnp.stack([(column // NA) * NA + neighbours[column % NA, j] for j in range(4)], 0).astype(jnp.int32)

    def one_point(krow):
        def step(acc, q):
            p = krow[q]
            s = shift[q]
            block = lax.dynamic_index_in_dim(padded, p, 0, keepdims=False)
            early = lax.dynamic_slice_in_dim(block, ((HALO - s) * NA).astype(jnp.int32), cols, 2)
            late = lax.dynamic_slice_in_dim(block, ((HALO + s) * NA).astype(jnp.int32), cols, 2)
            mix = (emit_weight[q] * early.astype(jnp.float32) + absorb_weight[q] * late.astype(jnp.float32)).astype(jnp.bfloat16)
            stacked = jnp.take(mix, index, axis=2).astype(jnp.float32)
            kq = lax.dynamic_index_in_dim(coupling, q, 0, keepdims=False).reshape(4, BLK, BLK).astype(jnp.float32)
            return acc + jnp.einsum('jmn,rnjc->rmc', kq, stacked), None

        start = jnp.zeros((2, BLK, cols), jnp.float32)
        acc, unused = lax.scan(step, start, jnp.arange(NK, dtype=jnp.int32))
        return acc

    return lax.map(one_point, kdiff)
```

```python
import jax
import jax.numpy as jnp
from jax import lax
from jax.experimental import pallas as pl
from jax.experimental.pallas import tpu as pltpu
from jax.sharding import PartitionSpec as P

BLK = 144
LANES = 128
NA = 16
NK = 32
SPAN = 16 * BLK
DEPTH = 8 * BLK
MESH = pl.DeviceIdType.MESH
BF16 = jnp.bfloat16
F32 = jnp.float32


def relay_couple(cbuf, cmain, ctail, head, tail, spread, j):
    @pl.loop(0, BLK // 16)
    def _(t):
        chunk = j * (BLK // 16) + t
        base = pl.multiple_of(chunk * SPAN, LANES)
        row = pl.multiple_of(chunk * 16, 16)
        for half in range(NK // 16):
            x = cbuf[16 * half : 16 * half + 16, pl.ds(base, SPAN)]
            for m in range(16):
                o = m * BLK
                a = x[:, o : o + LANES].astype(F32)
                b = x[:, o + LANES : o + BLK].astype(F32)
                for u in range(2):
                    r0 = ((2 * half + u) * 16 + m) * 8
                    head[r0 : r0 + 8, :] = a[8 * u : 8 * u + 8]
                    tail[r0 : r0 + 8, 0:16] = b[8 * u : 8 * u + 8]
            ends = []
            for u in range(2):
                for v in range(8):
                    q = 16 * half + 8 * u + v
                    rows = pl.ds((2 * half + u) * 128 + v, 16, stride=8)
                    cmain[q, pl.ds(row, 16), :] = head[rows, :].astype(BF16)
                    ends.append(tail[rows, :].astype(BF16))
            wide = jnp.dot(jnp.concatenate(ends, 0), spread, preferred_element_type=F32)
            for v in range(16):
                ctail[16 * half + v, pl.ds(row, 16), :] = wide[16 * v : 16 * v + 16].astype(BF16)


def shift_tables(table, before, own, after):
    for s in range(1, 8):
        w = NA * s
        table[s] = jnp.concatenate([before[:, LANES - w :], own[:, : LANES - w]], 1)
        table[8 + s] = jnp.concatenate([own[:, w:], after[:, :w]], 1)
    table[0] = before
    table[8] = after


def invert(kd, first):
    lane = lax.broadcasted_iota(jnp.int32, (NK, NK), 1)
    wide = lax.broadcasted_iota(jnp.int32, (NK, LANES), 1)
    result = jnp.zeros((NK, LANES), jnp.int32)
    for i in range(8):
        q = jnp.sum(jnp.where(kd == first + i, lane, 0), axis=1, keepdims=True)
        result = jnp.where(wide == i, jnp.minimum(q, NK - 1), result)
    return result


def sources(nbr, j):
    lane = lax.broadcasted_iota(jnp.int32, (8, LANES), 1)
    atom = lane % NA
    source = lane - atom
    for a in range(NA):
        source = jnp.where(atom == a, source + nbr[j, a], source)
    return source


def kernel(
    green, couple, kdiff, shift_in, emit_in, absorb_in, nbr_in, out,
    own, cbuf, cmain, ctail, head, tail, got, tab, rhs, mine, sendbuf, recvbuf, lanes_from, proj,
    kd, invv, inv, shift, emit, absorb, nbr,
    csem, lsem, gs, gr, rs, rr,
):
    kz, en = lax.axis_index("kz"), lax.axis_index("en")
    count = lax.axis_size("en")
    x, g = kz // 4, kz % 4
    h, c = g // 2, g % 2
    partner = (kz + 1 - 2 * c, en)
    across = (kz + 2 - 4 * h, en)
    later = (kz, (en + 1) % count)
    earlier = (kz, (en + count - 1) % count)

    def column(d):
        return ((kz + 4 * d) % 16, en)

    def fetch(j):
        cols = pl.ds(j * BLK * BLK, BLK * BLK)
        return pltpu.make_async_copy(couple.at[:, cols], cbuf.at[:, cols], csem.at[j])

    barrier = pltpu.get_barrier_semaphore()
    for peer in (partner, across, later, earlier, column(1), column(2), column(3)):
        pl.semaphore_signal(barrier, inc=1, device_id=peer, device_id_type=MESH)
    loads = [
        pltpu.make_async_copy(src, dst, lsem.at[n])
        for n, (src, dst) in enumerate(
            ((kdiff, kd), (shift_in, shift), (emit_in, emit), (absorb_in, absorb), (nbr_in, nbr), (green, own))
        )
    ]
    for load in loads:
        load.start()
    for j in range(4):
        fetch(j).start()
    tail[...] = jnp.zeros_like(tail)
    pl.semaphore_wait(barrier, 7)

    def hop(n, src, dst, peer):
        return pltpu.make_async_remote_copy(
            src_ref=src, dst_ref=dst, send_sem=gs.at[n], recv_sem=gr.at[n],
            device_id=peer, device_id_type=MESH,
        )

    hops = [
        hop(0, green, got.at[2, 1], across),
        hop(1, green, got.at[0, 0], later),
        hop(2, green, got.at[0, 2], earlier),
        hop(3, green, got.at[1, 1], partner),
        hop(4, got.at[2, 1], got.at[2, 0], later),
        hop(5, got.at[2, 1], got.at[2, 2], earlier),
        hop(6, got.at[2, 1], got.at[3, 1], partner),
        hop(7, got.at[0, 0], got.at[1, 0], partner),
        hop(8, got.at[0, 2], got.at[1, 2], partner),
        hop(9, got.at[2, 0], got.at[3, 0], partner),
        hop(10, got.at[2, 2], got.at[3, 2], partner),
    ]
    for n in range(4):
        hops[n].start()
    for load in loads:
        load.wait()
    invv[...] = invert(kd[...], 8 * x)
    to_scalar = pltpu.make_async_copy(invv, inv, lsem.at[0])
    to_scalar.start()
    for j in range(4):
        lanes_from[j] = sources(nbr, j)

    def tables(rho):
        @pl.loop(0, 4)
        def _(ir):
            i, r = ir // 2, ir % 2
            here = own[i, r] if rho == 0 else got[rho, 1, i, r]
            before, after = got[rho, 0, i, r], got[rho, 2, i, r]
            before = jnp.where(en > 0, before, jnp.zeros_like(before))
            after = jnp.where(en < count - 1, after, jnp.zeros_like(after))
            shift_tables(tab.at[2 * rho + i, :, r], before, here, after)

    fine = lax.broadcasted_iota(jnp.int32, (LANES, LANES), 1) % 16
    spread = jnp.where(lax.broadcasted_iota(jnp.int32, (LANES, LANES), 0) == fine, 1.0, 0.0).astype(BF16)

    def relay(j):
        fetch(j).wait()
        relay_couple(cbuf, cmain, ctail, head, tail, spread, j)

    relay(0)
    hops[0].wait_recv()
    for n in (4, 5, 6):
        hops[n].start()
    hops[1].wait_recv()
    hops[7].start()
    hops[2].wait_recv()
    hops[8].start()
    for j in range(1, 4):
        relay(j)
    hops[4].wait_recv()
    hops[9].start()
    hops[5].wait_recv()
    hops[10].start()
    tables(0)
    hops[3].wait_recv()
    hops[7].wait_recv()
    hops[8].wait_recv()
    tables(1)
    tables(2)
    hops[6].wait_recv()
    hops[9].wait_recv()
    hops[10].wait_recv()
    tables(3)
    to_scalar.wait()

    places = []
    for rho in range(4):
        owner = 2 * ((h + rho // 2) % 2) + (c + rho % 2) % 2
        for i in range(2):
            places.append(2 * owner + i)
    group = lax.broadcasted_iota(jnp.int32, (4 * BLK, LANES), 1) // 16

    def ring(dd):
        return pltpu.make_async_remote_copy(
            src_ref=sendbuf.at[dd], dst_ref=recvbuf.at[dd],
            send_sem=rs.at[dd], recv_sem=rr.at[dd],
            device_id=column(dd + 1), device_id_type=MESH,
        )

    def phonons_of(dd, kk):
        k = 8 * ((x + dd + 1) % 4) + 2 * g + kk
        return [inv[k, place] for place in places]

    def prepare(dd, kk):
        for slot, q in enumerate(phonons_of(dd, kk)):
            s = shift[q] % 8
            early = tab[slot, s].astype(F32)
            late = tab[slot, 8 + s].astype(F32)
            mix = (emit[q] * early + absorb[q] * late).astype(BF16)
            for r in range(2):
                lanes = slice(r * LANES, (r + 1) * LANES)
                rhs[kk, slot * LANES : (slot + 1) * LANES, lanes] = mix[r, :LANES]
                rhs[kk, 8 * LANES + slot * 16 : 8 * LANES + (slot + 1) * 16, lanes] = mix[r, LANES:]

    def project(dd, kk):
        phonons = phonons_of(dd, kk)
        last = ctail[phonons[0]]
        for slot in range(1, 8):
            last = jnp.where(group == slot, ctail[phonons[slot]], last)
        lhs = jnp.concatenate([cmain[q] for q in phonons] + [last], axis=1)
        proj[kk] = jnp.dot(lhs, rhs[kk], preferred_element_type=F32)

    def gather(dd):
        for kk in range(2):
            for r in range(2):
                for m in range(0, BLK, 8):
                    total = None
                    for j in range(4):
                        piece = proj[kk, j * BLK + m : j * BLK + m + 8, r * LANES : (r + 1) * LANES]
                        piece = jnp.take_along_axis(piece, lanes_from[j], axis=1, mode="promise_in_bounds")
                        total = piece if total is None else total + piece
                    mine[kk, r, m : m + 8] = total
                sendbuf[dd, kk, r] = mine[kk, r].astype(BF16)

    prepare(0, 0)
    prepare(0, 1)
    project(0, 0)
    prepare(1, 0)
    project(0, 1)

    @pl.loop(1, 4)
    def _(dd):
        gather(dd - 1)
        prepare(dd, 1)
        project(dd, 0)
        prepare(dd + 1, 0)
        project(dd, 1)
        ring(dd - 1).start()

    gather(3)
    for n in range(11):
        hops[n].wait_send()
    for dd in range(3):
        ring(dd).wait_recv()
    for kk in range(2):
        for r in range(2):
            out[kk, r] = mine[kk, r] + (
                recvbuf[0, kk, r].astype(F32)
                + recvbuf[1, kk, r].astype(F32)
                + recvbuf[2, kk, r].astype(F32)
            )
    for dd in range(3):
        ring(dd).wait_send()


def on_device(green, coupling, kdiff, shift, emit_weight, absorb_weight, neighbours):
    hbm = pl.BlockSpec(memory_space=pl.ANY)
    block = (2, 2, BLK, LANES)
    return pl.pallas_call(
        kernel,
        out_shape=jax.ShapeDtypeStruct(green.shape, F32),
        in_specs=[hbm] * 7,
        out_specs=pl.BlockSpec(memory_space=pltpu.VMEM),
        scratch_shapes=[
            pltpu.VMEM(block, BF16),
            pltpu.VMEM((NK, 4 * BLK * BLK), BF16),
            pltpu.VMEM((NK, 4 * BLK, LANES), BF16),
            pltpu.VMEM((NK, 4 * BLK, LANES), BF16),
            pltpu.VMEM((512, LANES), F32),
            pltpu.VMEM((512, LANES), F32),
            pltpu.VMEM((4, 3) + block, BF16),
            pltpu.VMEM((8, 16, 2, BLK, LANES), BF16),
            pltpu.VMEM((2, DEPTH, 2 * LANES), BF16),
            pltpu.VMEM(block, F32),
            pltpu.VMEM((4,) + block, BF16),
            pltpu.VMEM((3,) + block, BF16),
            pltpu.VMEM((4, 8, LANES), jnp.int32),
            pltpu.VMEM((2, 4 * BLK, 2 * LANES), F32),
            pltpu.VMEM((NK, NK), jnp.int32),
            pltpu.VMEM((NK, LANES), jnp.int32),
            pltpu.SMEM((NK, LANES), jnp.int32),
            pltpu.SMEM((NK,), jnp.int32),
            pltpu.SMEM((NK,), F32),
            pltpu.SMEM((NK,), F32),
            pltpu.SMEM((4, NA), jnp.int32),
            pltpu.SemaphoreType.DMA((4,)),
            pltpu.SemaphoreType.DMA((6,)),
            pltpu.SemaphoreType.DMA((11,)),
            pltpu.SemaphoreType.DMA((11,)),
            pltpu.SemaphoreType.DMA((3,)),
            pltpu.SemaphoreType.DMA((3,)),
        ],
        compiler_params=pltpu.CompilerParams(
            collective_id=0, has_side_effects=True, vmem_limit_bytes=62 * 2**20
        ),
    )(green, coupling, kdiff, shift, emit_weight, absorb_weight, neighbours.T)


def solution(mesh):
    return jax.shard_map(
        on_device,
        mesh=mesh,
        in_specs=(P("kz", None, None, "en"), P(), P(), P(), P(), P(), P()),
        out_specs=P("kz", None, None, "en"),
        check_vma=False,
    )
```

```python
import jax
import jax.numpy as jnp
from jax import lax
from jax.experimental import pallas as pl
from jax.experimental.pallas import tpu as pltpu
from jax.sharding import PartitionSpec as P

BLK = 144
LANES = 128
NA = 16
NK = 32
SPAN = 16 * BLK
FOLD = 3
MESH = pl.DeviceIdType.MESH
BF16 = jnp.bfloat16
F32 = jnp.float32


def relay_couple(cbuf, cmain, ctail, head, tail, spread, part):
    for f in range(FOLD):
        chunk = part * FOLD + f
        base = chunk * SPAN
        row = chunk * 16
        if not isinstance(part, int):
            base, row = pl.multiple_of(base, LANES), pl.multiple_of(row, 16)
        for half in range(NK // 16):
            x = cbuf[16 * half : 16 * half + 16, pl.ds(base, SPAN)]
            for m in range(16):
                o = m * BLK
                a = x[:, o : o + LANES].astype(F32)
                b = x[:, o + LANES : o + BLK].astype(F32)
                for u in range(2):
                    r0 = ((2 * half + u) * 16 + m) * 8
                    head[f, r0 : r0 + 8, :] = a[8 * u : 8 * u + 8]
                    tail[f, r0 : r0 + 8, 0:16] = b[8 * u : 8 * u + 8]
            tips = []
            for u in range(2):
                for v in range(8):
                    q = 16 * half + 8 * u + v
                    rows = pl.ds((2 * half + u) * 128 + v, 16, stride=8)
                    cmain[q, pl.ds(row, 16), :] = head[f, rows, :].astype(BF16)
                    tips.append(tail[f, rows, :].astype(BF16))
            wide = jnp.dot(jnp.concatenate(tips, 0), spread, preferred_element_type=F32)
            for v in range(16):
                ctail[16 * half + v, pl.ds(row, 16), :] = wide[16 * v : 16 * v + 16].astype(BF16)


def shift_tables(table, before, own, after):
    for s in range(1, 8):
        w = NA * s
        table[s] = jnp.concatenate([before[:, LANES - w :], own[:, : LANES - w]], 1)
        table[8 + s] = jnp.concatenate([own[:, w:], after[:, :w]], 1)
    table[0] = before
    table[8] = after


def invert(kd, first):
    lane = lax.broadcasted_iota(jnp.int32, (NK, NK), 1)
    wide = lax.broadcasted_iota(jnp.int32, (NK, LANES), 1)
    result = jnp.zeros((NK, LANES), jnp.int32)
    for i in range(8):
        q = jnp.sum(jnp.where(kd == first + i, lane, 0), axis=1, keepdims=True)
        result = jnp.where(wide == i, jnp.minimum(q, NK - 1), result)
    return result


def sources(nbr, j):
    lane = lax.broadcasted_iota(jnp.int32, (8, LANES), 1)
    atom = lane % NA
    source = lane - atom
    for a in range(NA):
        source = jnp.where(atom == a, source + nbr[j, a], source)
    return source


def kernel(
    green, couple, kdiff, shift_in, emit_in, absorb_in, nbr_in, out,
    own, cbuf, cmain, ctail, head, tail, got, tab, rhs, ends, mine, sendbuf, recvbuf, lanes_from, proj,
    kd, invv, inv, shift, emit, absorb, nbr,
    csem, lsem, gs, gr, rs, rr,
):
    kz, en = lax.axis_index("kz"), lax.axis_index("en")
    count = lax.axis_size("en")
    x, g = kz // 4, kz % 4
    h, c = g // 2, g % 2
    partner = (kz + 1 - 2 * c, en)
    across = (kz + 2 - 4 * h, en)
    later = (kz, (en + 1) % count)
    earlier = (kz, (en + count - 1) % count)

    def column(d):
        return ((kz + 4 * d) % 16, en)

    def fetch(j):
        cols = pl.ds(j * BLK * BLK, BLK * BLK)
        return pltpu.make_async_copy(couple.at[:, cols], cbuf.at[:, cols], csem.at[j])

    barrier = pltpu.get_barrier_semaphore()
    for peer in (partner, across, later, earlier, column(1), column(2), column(3)):
        pl.semaphore_signal(barrier, inc=1, device_id=peer, device_id_type=MESH)
    loads = [
        pltpu.make_async_copy(src, dst, lsem.at[n])
        for n, (src, dst) in enumerate(
            ((kdiff, kd), (shift_in, shift), (emit_in, emit), (absorb_in, absorb), (nbr_in, nbr), (green, own))
        )
    ]
    for load in loads:
        load.start()
    for j in range(4):
        fetch(j).start()
    tail[...] = jnp.zeros_like(tail)
    pl.semaphore_wait(barrier, 7)

    def hop(n, src, dst, peer):
        return [
            pltpu.make_async_remote_copy(
                src_ref=src.at[i], dst_ref=dst.at[i],
                send_sem=gs.at[2 * n + i], recv_sem=gr.at[2 * n + i],
                device_id=peer, device_id_type=MESH,
            )
            for i in range(2)
        ]

    hops = [
        hop(0, green, got.at[2, 1], across),
        hop(1, green, got.at[0, 0], later),
        hop(2, green, got.at[0, 2], earlier),
        hop(3, green, got.at[1, 1], partner),
        hop(4, got.at[2, 1], got.at[2, 0], later),
        hop(5, got.at[2, 1], got.at[2, 2], earlier),
        hop(6, got.at[2, 1], got.at[3, 1], partner),
        hop(7, got.at[0, 0], got.at[1, 0], partner),
        hop(8, got.at[0, 2], got.at[1, 2], partner),
        hop(9, got.at[2, 0], got.at[3, 0], partner),
        hop(10, got.at[2, 2], got.at[3, 2], partner),
    ]

    def forward(n, onward, i):
        hops[n][i].wait_recv()
        for target in onward:
            hops[target][i].start()

    for i in range(2):
        for n in range(4):
            hops[n][i].start()
    for load in loads:
        load.wait()
    invv[...] = invert(kd[...], 8 * x)
    to_scalar = pltpu.make_async_copy(invv, inv, lsem.at[0])
    to_scalar.start()
    for j in range(4):
        lanes_from[j] = sources(nbr, j)

    def table(rho, ir):
        i, r = ir // 2, ir % 2
        here = own[i, r] if rho == 0 else got[rho, 1, i, r]
        before, after = got[rho, 0, i, r], got[rho, 2, i, r]
        before = jnp.where(en > 0, before, jnp.zeros_like(before))
        after = jnp.where(en < count - 1, after, jnp.zeros_like(after))
        shift_tables(tab.at[2 * rho + i, :, r], before, here, after)

    def tables(rho):
        @pl.loop(0, 4)
        def _(ir):
            table(rho, ir)

    fine = lax.broadcasted_iota(jnp.int32, (LANES, LANES), 1) % 16
    spread = jnp.where(lax.broadcasted_iota(jnp.int32, (LANES, LANES), 0) == fine, 1.0, 0.0).astype(BF16)

    def relay(first, last):
        for j in range(4):
            if first <= j * 36 // (4 * FOLD) < last:
                fetch(j).wait()

        @pl.loop(first, last)
        def _(part):
            relay_couple(cbuf, cmain, ctail, head, tail, spread, part)

    relay(0, 4)
    forward(0, (4, 5, 6), 0)
    relay(4, 6)
    forward(1, (7,), 0)
    forward(2, (8,), 0)
    forward(0, (4, 5, 6), 1)
    relay(6, 8)
    forward(1, (7,), 1)
    forward(2, (8,), 1)
    relay(8, 12)
    forward(4, (9,), 0)
    forward(5, (10,), 0)
    tables(0)
    forward(4, (9,), 1)
    forward(5, (10,), 1)
    for n in (3, 7, 8):
        for i in range(2):
            forward(n, (), i)
    tables(1)
    to_scalar.wait()

    places = []
    for rho in range(4):
        owner = 2 * ((h + rho // 2) % 2) + (c + rho % 2) % 2
        for i in range(2):
            places.append(2 * owner + i)
    group = lax.broadcasted_iota(jnp.int32, (4 * BLK, LANES), 1) // 16

    def ring(dd):
        return pltpu.make_async_remote_copy(
            src_ref=sendbuf.at[dd], dst_ref=recvbuf.at[dd],
            send_sem=rs.at[dd], recv_sem=rr.at[dd],
            device_id=column(dd + 1), device_id_type=MESH,
        )

    def phonons_of(dd, kk):
        k = 8 * ((x + dd + 1) % 4) + 2 * g + kk
        return [inv[k, place] for place in places]

    def prepare(dd, kk, half):
        for slot, q in enumerate(phonons_of(dd, kk)):
            if slot // 4 != half:
                continue
            s = shift[q] % 8
            early = tab[slot, s].astype(F32)
            late = tab[slot, 8 + s].astype(F32)
            mix = (emit[q] * early + absorb[q] * late).astype(BF16)
            for r in range(2):
                lanes = slice(r * LANES, (r + 1) * LANES)
                rhs[kk, slot % 4 * LANES : (slot % 4 + 1) * LANES, lanes] = mix[r, :LANES]
                ends[dd % 4, kk, slot * 16 : (slot + 1) * 16, lanes] = mix[r, LANES:]

    def project(dd, kk, half):
        phonons = phonons_of(dd, kk)
        lhs = jnp.concatenate([cmain[q] for q in phonons[4 * half : 4 * half + 4]], axis=1)
        part = jnp.dot(lhs, rhs[kk], preferred_element_type=F32)
        if half == 0:
            proj[dd, kk] = part
            return
        last = ctail[phonons[0]]
        for slot in range(1, 8):
            last = jnp.where(group == slot, ctail[phonons[slot]], last)
        part = part + jnp.dot(last, ends[dd, kk], preferred_element_type=F32)
        proj[dd, kk] = proj[dd, kk] + part

    def gather(dd):
        for kk in range(2):
            for r in range(2):
                for m in range(0, BLK, 8):
                    total = None
                    for j in range(4):
                        piece = proj[dd, kk, j * BLK + m : j * BLK + m + 8, r * LANES : (r + 1) * LANES]
                        piece = jnp.take_along_axis(piece, lanes_from[j], axis=1, mode="promise_in_bounds")
                        total = piece if total is None else total + piece
                    mine[kk, r, m : m + 8] = total
                sendbuf[dd, kk, r] = mine[kk, r].astype(BF16)

    prepare(0, 0, 0)

    @pl.loop(0, 4)
    def _(dd):
        prepare(dd, 1, 0)
        project(dd, 0, 0)
        table(2, dd)
        prepare(dd + 1, 0, 0)
        project(dd, 1, 0)

    for n in (6, 9, 10):
        for i in range(2):
            forward(n, (), i)
    tables(3)
    prepare(0, 0, 1)
    prepare(0, 1, 1)
    project(0, 0, 1)
    prepare(1, 0, 1)
    project(0, 1, 1)

    @pl.loop(1, 4)
    def _(dd):
        gather(dd - 1)
        prepare(dd, 1, 1)
        project(dd, 0, 1)
        prepare(dd + 1, 0, 1)
        project(dd, 1, 1)
        ring(dd - 1).start()

    gather(3)
    for pair in hops:
        for piece in pair:
            piece.wait_send()
    for dd in range(3):
        ring(dd).wait_recv()
    for kk in range(2):
        for r in range(2):
            out[kk, r] = mine[kk, r] + (
                recvbuf[0, kk, r].astype(F32)
                + recvbuf[1, kk, r].astype(F32)
                + recvbuf[2, kk, r].astype(F32)
            )
    for dd in range(3):
        ring(dd).wait_send()


def on_device(green, coupling, kdiff, shift, emit_weight, absorb_weight, neighbours):
    hbm = pl.BlockSpec(memory_space=pl.ANY)
    block = (2, 2, BLK, LANES)
    return pl.pallas_call(
        kernel,
        out_shape=jax.ShapeDtypeStruct(green.shape, F32),
        in_specs=[hbm] * 7,
        out_specs=pl.BlockSpec(memory_space=pltpu.VMEM),
        scratch_shapes=[
            pltpu.VMEM(block, BF16),
            pltpu.VMEM((NK, 4 * BLK * BLK), BF16),
            pltpu.VMEM((NK, 4 * BLK, LANES), BF16),
            pltpu.VMEM((NK, 4 * BLK, LANES), BF16),
            pltpu.VMEM((FOLD, 512, LANES), F32),
            pltpu.VMEM((FOLD, 512, LANES), F32),
            pltpu.VMEM((4, 3) + block, BF16),
            pltpu.VMEM((8, 16, 2, BLK, LANES), BF16),
            pltpu.VMEM((2, 4 * LANES, 2 * LANES), BF16),
            pltpu.VMEM((4, 2, LANES, 2 * LANES), BF16),
            pltpu.VMEM(block, F32),
            pltpu.VMEM((4,) + block, BF16),
            pltpu.VMEM((3,) + block, BF16),
            pltpu.VMEM((4, 8, LANES), jnp.int32),
            pltpu.VMEM((4, 2, 4 * BLK, 2 * LANES), F32),
            pltpu.VMEM((NK, NK), jnp.int32),
            pltpu.VMEM((NK, LANES), jnp.int32),
            pltpu.SMEM((NK, LANES), jnp.int32),
            pltpu.SMEM((NK,), jnp.int32),
            pltpu.SMEM((NK,), F32),
            pltpu.SMEM((NK,), F32),
            pltpu.SMEM((4, NA), jnp.int32),
            pltpu.SemaphoreType.DMA((4,)),
            pltpu.SemaphoreType.DMA((6,)),
            pltpu.SemaphoreType.DMA((22,)),
            pltpu.SemaphoreType.DMA((22,)),
            pltpu.SemaphoreType.DMA((3,)),
            pltpu.SemaphoreType.DMA((3,)),
        ],
        compiler_params=pltpu.CompilerParams(
            collective_id=0, has_side_effects=True, vmem_limit_bytes=62 * 2**20
        ),
    )(green, coupling, kdiff, shift, emit_weight, absorb_weight, neighbours.T)


def solution(mesh):
    return jax.shard_map(
        on_device,
        mesh=mesh,
        in_specs=(P("kz", None, None, "en"), P(), P(), P(), P(), P(), P()),
        out_specs=P("kz", None, None, "en"),
        check_vma=False,
    )
```

```python
import jax
import jax.numpy as jnp
from jax import lax
from jax.experimental import pallas as pl
from jax.experimental.pallas import tpu as pltpu
from jax.sharding import PartitionSpec as P

BLK = 144
LANES = 128
NA = 16
NK = 32
SPAN = 16 * BLK
FOLD = 6
MESH = pl.DeviceIdType.MESH
BF16 = jnp.bfloat16
F32 = jnp.float32


def relay_couple(cbuf, cmain, ctail, head, tail, spread, part):
    for f in range(FOLD):
        chunk = part * FOLD + f
        base = chunk * SPAN
        row = chunk * 16
        if not isinstance(part, int):
            base, row = pl.multiple_of(base, LANES), pl.multiple_of(row, 16)
        for half in range(NK // 16):
            x = cbuf[16 * half : 16 * half + 16, pl.ds(base, SPAN)]
            for m in range(16):
                o = m * BLK
                a = x[:, o : o + LANES].astype(F32)
                b = x[:, o + LANES : o + BLK].astype(F32)
                for u in range(2):
                    r0 = ((2 * half + u) * 16 + m) * 8
                    head[f, r0 : r0 + 8, :] = a[8 * u : 8 * u + 8]
                    tail[f, r0 : r0 + 8, 0:16] = b[8 * u : 8 * u + 8]
            tips = []
            for u in range(2):
                for v in range(8):
                    q = 16 * half + 8 * u + v
                    rows = pl.ds((2 * half + u) * 128 + v, 16, stride=8)
                    cmain[q, pl.ds(row, 16), :] = head[f, rows, :].astype(BF16)
                    tips.append(tail[f, rows, :].astype(BF16))
            wide = jnp.dot(jnp.concatenate(tips, 0), spread, preferred_element_type=F32)
            for v in range(16):
                ctail[16 * half + v, pl.ds(row, 16), :] = wide[16 * v : 16 * v + 16].astype(BF16)


def shift_tables(table, before, own, after):
    for s in range(1, 8):
        w = NA * s
        table[s] = jnp.concatenate([before[:, LANES - w :], own[:, : LANES - w]], 1)
        table[8 + s] = jnp.concatenate([own[:, w:], after[:, :w]], 1)
    table[0] = before
    table[8] = after


def invert(kd, first):
    lane = lax.broadcasted_iota(jnp.int32, (NK, NK), 1)
    wide = lax.broadcasted_iota(jnp.int32, (NK, LANES), 1)
    result = jnp.zeros((NK, LANES), jnp.int32)
    for i in range(8):
        q = jnp.sum(jnp.where(kd == first + i, lane, 0), axis=1, keepdims=True)
        result = jnp.where(wide == i, jnp.minimum(q, NK - 1), result)
    return result


def sources(nbr, j):
    lane = lax.broadcasted_iota(jnp.int32, (8, LANES), 1)
    atom = lane % NA
    source = lane - atom
    for a in range(NA):
        source = jnp.where(atom == a, source + nbr[j, a], source)
    return source


def kernel(
    green, couple, kdiff, shift_in, emit_in, absorb_in, nbr_in, mine_out, recvbuf,
    own, cbuf, cmain, ctail, head, tail, got, tab, rhs, ends, mine, sendbuf, lanes_from, proj,
    kd, invv, inv, shift, emit, absorb, nbr,
    csem, lsem, gs, gr, rs, rr,
):
    kz, en = lax.axis_index("kz"), lax.axis_index("en")
    count = lax.axis_size("en")
    x, g = kz // 4, kz % 4
    h, c = g // 2, g % 2
    partner = (kz + 1 - 2 * c, en)
    across = (kz + 2 - 4 * h, en)
    later = (kz, (en + 1) % count)
    earlier = (kz, (en + count - 1) % count)

    def order(dd):
        return (2 + 3 * dd + 3 * (dd // 2) + 2 * (dd // 3)) % 4

    def column(d):
        return ((kz + 4 * d) % 16, en)

    def fetch(j):
        cols = pl.ds(j * BLK * BLK, BLK * BLK)
        return pltpu.make_async_copy(couple.at[:, cols], cbuf.at[:, cols], csem.at[j])

    barrier = pltpu.get_barrier_semaphore()
    for peer in (partner, across, later, earlier, column(1), column(2), column(3)):
        pl.semaphore_signal(barrier, inc=1, device_id=peer, device_id_type=MESH)
    loads = [
        pltpu.make_async_copy(src, dst, lsem.at[n])
        for n, (src, dst) in enumerate(
            ((kdiff, kd), (shift_in, shift), (emit_in, emit), (absorb_in, absorb), (nbr_in, nbr), (green, own))
        )
    ]
    for load in loads:
        load.start()
    for j in range(4):
        fetch(j).start()
    tail[...] = jnp.zeros_like(tail)
    pl.semaphore_wait(barrier, 7)

    def hop(n, src, dst, peer):
        return [
            pltpu.make_async_remote_copy(
                src_ref=src.at[i], dst_ref=dst.at[i],
                send_sem=gs.at[2 * n + i], recv_sem=gr.at[2 * n + i],
                device_id=peer, device_id_type=MESH,
            )
            for i in range(2)
        ]

    hops = [
        hop(0, green, got.at[2, 1], across),
        hop(1, green, got.at[0, 0], later),
        hop(2, green, got.at[0, 2], earlier),
        hop(3, green, got.at[1, 1], partner),
        hop(4, got.at[2, 1], got.at[2, 0], later),
        hop(5, got.at[2, 1], got.at[2, 2], earlier),
        hop(6, got.at[2, 1], got.at[3, 1], partner),
        hop(7, got.at[0, 0], got.at[1, 0], partner),
        hop(8, got.at[0, 2], got.at[1, 2], partner),
        hop(9, got.at[2, 0], got.at[3, 0], partner),
        hop(10, got.at[2, 2], got.at[3, 2], partner),
    ]

    def forward(n, onward, i):
        hops[n][i].wait_recv()
        for target in onward:
            hops[target][i].start()

    for i in range(2):
        for n in range(4):
            hops[n][i].start()
    for load in loads:
        load.wait()
    invv[...] = invert(kd[...], 8 * x)
    to_scalar = pltpu.make_async_copy(invv, inv, lsem.at[0])
    to_scalar.start()
    for j in range(4):
        lanes_from[j] = sources(nbr, j)

    def table(rho, i, r):
        here = own[i, r] if rho == 0 else got[rho, 1, i, r]
        before, after = got[rho, 0, i, r], got[rho, 2, i, r]
        before = jnp.where(en > 0, before, jnp.zeros_like(before))
        after = jnp.where(en < count - 1, after, jnp.zeros_like(after))
        shift_tables(tab.at[2 * rho + i, :, r], before, here, after)

    def tables(rho):
        @pl.loop(0, 2)
        def _(i):
            for r in range(2):
                table(rho, i, r)

    fine = lax.broadcasted_iota(jnp.int32, (LANES, LANES), 1) % 16
    spread = jnp.where(lax.broadcasted_iota(jnp.int32, (LANES, LANES), 0) == fine, 1.0, 0.0).astype(BF16)

    @pl.loop(0, BLK * 4 // 16 // FOLD)
    def _(part):
        for j, at in enumerate((0, 0, 3, 4)):
            @pl.when(part == at)
            def _():
                fetch(j).wait()

        relay_couple(cbuf, cmain, ctail, head, tail, spread, part)

        @pl.when(part == 1)
        def _():
            forward(0, (4, 5, 6), 0)

        @pl.when(part == 2)
        def _():
            forward(1, (7,), 0)
            forward(2, (8,), 0)
            forward(0, (4, 5, 6), 1)

        @pl.when(part == 3)
        def _():
            forward(1, (7,), 1)
            forward(2, (8,), 1)

    forward(4, (9,), 0)
    forward(5, (10,), 0)
    tables(0)
    forward(4, (9,), 1)
    forward(5, (10,), 1)
    for n in (3, 7, 8):
        for i in range(2):
            forward(n, (), i)
    tables(1)
    to_scalar.wait()

    places = []
    for rho in range(4):
        owner = 2 * ((h + rho // 2) % 2) + (c + rho % 2) % 2
        for i in range(2):
            places.append(2 * owner + i)
    group = lax.broadcasted_iota(jnp.int32, (4 * BLK, LANES), 1) // 16

    def ring(dd):
        return pltpu.make_async_remote_copy(
            src_ref=sendbuf.at[dd], dst_ref=recvbuf.at[dd],
            send_sem=rs.at[dd], recv_sem=rr.at[dd],
            device_id=column(order(dd)), device_id_type=MESH,
        )

    def phonons_of(dd, kk):
        k = 8 * ((x + order(dd % 4)) % 4) + 2 * g + kk
        return [inv[k, place] for place in places]

    def prepare(dd, kk, half):
        for slot, q in enumerate(phonons_of(dd, kk)):
            if slot // 4 != half:
                continue
            s = shift[q] % 8
            early = tab[slot, s].astype(F32)
            late = tab[slot, 8 + s].astype(F32)
            mix = (emit[q] * early + absorb[q] * late).astype(BF16)
            for r in range(2):
                lanes = slice(r * LANES, (r + 1) * LANES)
                rhs[kk, slot % 4 * LANES : (slot % 4 + 1) * LANES, lanes] = mix[r, :LANES]
                ends[dd % 4, kk, slot * 16 : (slot + 1) * 16, lanes] = mix[r, LANES:]

    def project(dd, kk, half):
        phonons = phonons_of(dd, kk)
        lhs = jnp.concatenate([cmain[q] for q in phonons[4 * half : 4 * half + 4]], axis=1)
        part = jnp.dot(lhs, rhs[kk], preferred_element_type=F32)
        if half == 0:
            proj[dd, kk] = part
            return
        last = ctail[phonons[0]]
        for slot in range(1, 8):
            last = jnp.where(group == slot, ctail[phonons[slot]], last)
        part = part + jnp.dot(last, ends[dd, kk], preferred_element_type=F32)
        proj[dd, kk] = proj[dd, kk] + part

    def gather(dd):
        for kk in range(2):
            for r in range(2):
                for m in range(0, BLK, 8):
                    total = None
                    for j in range(4):
                        piece = proj[dd, kk, j * BLK + m : j * BLK + m + 8, r * LANES : (r + 1) * LANES]
                        piece = jnp.take_along_axis(piece, lanes_from[j], axis=1, mode="promise_in_bounds")
                        total = piece if total is None else total + piece
                    mine[kk, r, m : m + 8] = total
                sendbuf[dd, kk, r] = mine[kk, r].astype(BF16)

    prepare(0, 0, 0)

    @pl.loop(0, 4)
    def _(dd):
        prepare(dd, 1, 0)
        project(dd, 0, 0)
        table(2, dd // 2, dd % 2)
        prepare(dd + 1, 0, 0)
        project(dd, 1, 0)

    for n in (6, 9, 10):
        for i in range(2):
            forward(n, (), i)
    tables(3)
    prepare(0, 0, 1)
    prepare(0, 1, 1)
    project(0, 0, 1)
    prepare(1, 0, 1)
    project(0, 1, 1)

    @pl.loop(1, 4)
    def _(dd):
        gather(dd - 1)
        prepare(dd, 1, 1)
        project(dd, 0, 1)
        prepare(dd + 1, 0, 1)
        project(dd, 1, 1)
        ring(dd - 1).start()

    gather(3)
    keep = pltpu.make_async_copy(mine, mine_out, lsem.at[1])
    keep.start()
    for pair in hops:
        for piece in pair:
            piece.wait_send()
    for dd in range(3):
        ring(dd).wait_send()
    keep.wait()
    for dd in range(3):
        ring(dd).wait_recv()


def on_device(green, coupling, kdiff, shift, emit_weight, absorb_weight, neighbours):
    hbm = pl.BlockSpec(memory_space=pl.ANY)
    block = (2, 2, BLK, LANES)
    total, parts = pl.pallas_call(
        kernel,
        out_shape=(jax.ShapeDtypeStruct(block, F32), jax.ShapeDtypeStruct((3,) + block, BF16)),
        in_specs=[hbm] * 7,
        out_specs=(hbm, hbm),
        scratch_shapes=[
            pltpu.VMEM(block, BF16),
            pltpu.VMEM((NK, 4 * BLK * BLK), BF16),
            pltpu.VMEM((NK, 4 * BLK, LANES), BF16),
            pltpu.VMEM((NK, 4 * BLK, LANES), BF16),
            pltpu.VMEM((FOLD, 512, LANES), F32),
            pltpu.VMEM((FOLD, 512, LANES), F32),
            pltpu.VMEM((4, 3) + block, BF16),
            pltpu.VMEM((8, 16, 2, BLK, LANES), BF16),
            pltpu.VMEM((2, 4 * LANES, 2 * LANES), BF16),
            pltpu.VMEM((4, 2, LANES, 2 * LANES), BF16),
            pltpu.VMEM(block, F32),
            pltpu.VMEM((4,) + block, BF16),
            pltpu.VMEM((4, 8, LANES), jnp.int32),
            pltpu.VMEM((4, 2, 4 * BLK, 2 * LANES), F32),
            pltpu.VMEM((NK, NK), jnp.int32),
            pltpu.VMEM((NK, LANES), jnp.int32),
            pltpu.SMEM((NK, LANES), jnp.int32),
            pltpu.SMEM((NK,), jnp.int32),
            pltpu.SMEM((NK,), F32),
            pltpu.SMEM((NK,), F32),
            pltpu.SMEM((4, NA), jnp.int32),
            pltpu.SemaphoreType.DMA((4,)),
            pltpu.SemaphoreType.DMA((6,)),
            pltpu.SemaphoreType.DMA((22,)),
            pltpu.SemaphoreType.DMA((22,)),
            pltpu.SemaphoreType.DMA((3,)),
            pltpu.SemaphoreType.DMA((3,)),
        ],
        compiler_params=pltpu.CompilerParams(
            collective_id=0, has_side_effects=True, vmem_limit_bytes=62 * 2**20
        ),
    )(green, coupling, kdiff, shift, emit_weight, absorb_weight, neighbours.T)
    return total + (parts[0].astype(F32) + parts[1].astype(F32) + parts[2].astype(F32))


def solution(mesh):
    return jax.shard_map(
        on_device,
        mesh=mesh,
        in_specs=(P("kz", None, None, "en"), P(), P(), P(), P(), P(), P()),
        out_specs=P("kz", None, None, "en"),
        check_vma=False,
    )
```

```python
import jax
import jax.numpy as jnp
from jax import lax
from jax.experimental import pallas as pl
from jax.experimental.pallas import tpu as pltpu
from jax.sharding import PartitionSpec as P

BLK = 144
LANES = 128
NA = 16
NK = 32
SPAN = 16 * BLK
FOLD = 6
MESH = pl.DeviceIdType.MESH
BF16 = jnp.bfloat16
F32 = jnp.float32


def relay_couple(cbuf, cmain, ctail, head, tail, spread, part):
    for f in range(FOLD):
        chunk = part * FOLD + f
        base = chunk * SPAN
        row = chunk * 16
        if not isinstance(part, int):
            base, row = pl.multiple_of(base, LANES), pl.multiple_of(row, 16)
        for half in range(NK // 16):
            x = cbuf[16 * half : 16 * half + 16, pl.ds(base, SPAN)]
            for m in range(16):
                o = m * BLK
                a = x[:, o : o + LANES].astype(F32)
                b = x[:, o + LANES : o + BLK].astype(F32)
                for u in range(2):
                    r0 = ((2 * half + u) * 16 + m) * 8
                    head[f, r0 : r0 + 8, :] = a[8 * u : 8 * u + 8]
                    tail[f, r0 : r0 + 8, 0:16] = b[8 * u : 8 * u + 8]
            tips = []
            for u in range(2):
                for v in range(8):
                    q = 16 * half + 8 * u + v
                    rows = pl.ds((2 * half + u) * 128 + v, 16, stride=8)
                    cmain[q, pl.ds(row, 16), :] = head[f, rows, :].astype(BF16)
                    tips.append(tail[f, rows, :].astype(BF16))
            wide = jnp.dot(jnp.concatenate(tips, 0), spread, preferred_element_type=F32)
            for v in range(16):
                ctail[16 * half + v, pl.ds(row, 16), :] = wide[16 * v : 16 * v + 16].astype(BF16)


def shift_tables(table, before, own, after):
    for s in range(1, 8):
        w = NA * s
        table[s] = jnp.concatenate([before[:, LANES - w :], own[:, : LANES - w]], 1)
        table[8 + s] = jnp.concatenate([own[:, w:], after[:, :w]], 1)
    table[0] = before
    table[8] = after


def invert(kd, first):
    lane = lax.broadcasted_iota(jnp.int32, (NK, NK), 1)
    wide = lax.broadcasted_iota(jnp.int32, (NK, LANES), 1)
    result = jnp.zeros((NK, LANES), jnp.int32)
    for i in range(8):
        q = jnp.sum(jnp.where(kd == first + i, lane, 0), axis=1, keepdims=True)
        result = jnp.where(wide == i, jnp.minimum(q, NK - 1), result)
    return result


def sources(nbr, j):
    lane = lax.broadcasted_iota(jnp.int32, (8, LANES), 1)
    atom = lane % NA
    source = lane - atom
    for a in range(NA):
        source = jnp.where(atom == a, source + nbr[j, a], source)
    return source


def kernel(
    green, couple, kdiff, shift_in, emit_in, absorb_in, nbr_in, mine_out, recvbuf,
    own, cbuf, cmain, ctail, head, tail, got, tab, rhs, ends, mine, sendbuf, lanes_from, proj,
    kd, invv, inv, shift, emit, absorb, nbr,
    csem, lsem, gs, gr, rs, rr,
):
    kz, en = lax.axis_index("kz"), lax.axis_index("en")
    count = lax.axis_size("en")
    x, g = kz // 4, kz % 4
    h, c = g // 2, g % 2
    partner = (kz + 1 - 2 * c, en)
    across = (kz + 2 - 4 * h, en)
    later = (kz, (en + 1) % count)
    earlier = (kz, (en + count - 1) % count)

    def order(dd):
        return (2 + 3 * dd + 3 * (dd // 2) + 2 * (dd // 3)) % 4

    def column(d):
        return ((kz + 4 * d) % 16, en)

    def fetch(j):
        cols = pl.ds(j * BLK * BLK, BLK * BLK)
        return pltpu.make_async_copy(couple.at[:, cols], cbuf.at[:, cols], csem.at[j])

    barrier = pltpu.get_barrier_semaphore()
    for peer in (partner, across, later, earlier, column(1), column(2), column(3)):
        pl.semaphore_signal(barrier, inc=1, device_id=peer, device_id_type=MESH)
    loads = [
        pltpu.make_async_copy(src, dst, lsem.at[n])
        for n, (src, dst) in enumerate(
            ((kdiff, kd), (shift_in, shift), (emit_in, emit), (absorb_in, absorb), (nbr_in, nbr), (green, own))
        )
    ]
    for load in loads:
        load.start()
    for j in range(4):
        fetch(j).start()
    tail[...] = jnp.zeros_like(tail)
    pl.semaphore_wait(barrier, 7)

    def hop(n, src, dst, peer):
        return [
            pltpu.make_async_remote_copy(
                src_ref=src.at[i], dst_ref=dst.at[i],
                send_sem=gs.at[2 * n + i], recv_sem=gr.at[2 * n + i],
                device_id=peer, device_id_type=MESH,
            )
            for i in range(2)
        ]

    hops = [
        hop(0, green, got.at[2, 1], across),
        hop(1, green, got.at[0, 0], later),
        hop(2, green, got.at[0, 2], earlier),
        hop(3, green, got.at[1, 1], partner),
        hop(4, got.at[2, 1], got.at[2, 0], later),
        hop(5, got.at[2, 1], got.at[2, 2], earlier),
        hop(6, got.at[2, 1], got.at[3, 1], partner),
        hop(7, got.at[0, 0], got.at[1, 0], partner),
        hop(8, got.at[0, 2], got.at[1, 2], partner),
        hop(9, got.at[2, 0], got.at[3, 0], partner),
        hop(10, got.at[2, 2], got.at[3, 2], partner),
    ]

    def forward(n, onward, i):
        hops[n][i].wait_recv()
        for target in onward:
            hops[target][i].start()

    for i in range(2):
        for n in range(4):
            hops[n][i].start()
    for load in loads:
        load.wait()
    invv[...] = invert(kd[...], 8 * x)
    to_scalar = pltpu.make_async_copy(invv, inv, lsem.at[0])
    to_scalar.start()
    for j in range(4):
        lanes_from[j] = sources(nbr, j)

    def table(rho, i, r):
        here = own[i, r] if rho == 0 else got[rho, 1, i, r]
        before, after = got[rho, 0, i, r], got[rho, 2, i, r]
        before = jnp.where(en > 0, before, jnp.zeros_like(before))
        after = jnp.where(en < count - 1, after, jnp.zeros_like(after))
        shift_tables(tab.at[2 * rho + i, :, r], before, here, after)

    def tables(rho):
        @pl.loop(0, 2)
        def _(i):
            for r in range(2):
                table(rho, i, r)

    fine = lax.broadcasted_iota(jnp.int32, (LANES, LANES), 1) % 16
    spread = jnp.where(lax.broadcasted_iota(jnp.int32, (LANES, LANES), 0) == fine, 1.0, 0.0).astype(BF16)

    @pl.loop(0, BLK * 4 // 16 // FOLD)
    def _(part):
        for j, at in enumerate((0, 0, 3, 4)):
            @pl.when(part == at)
            def _():
                fetch(j).wait()

        relay_couple(cbuf, cmain, ctail, head, tail, spread, part)

        @pl.when(part == 1)
        def _():
            forward(0, (4, 5, 6), 0)

        @pl.when(part == 2)
        def _():
            forward(1, (7,), 0)
            forward(2, (8,), 0)

        @pl.when(part == 3)
        def _():
            forward(0, (4, 5, 6), 1)
            forward(1, (7,), 1)
            forward(2, (8,), 1)

    forward(4, (9,), 0)
    forward(5, (10,), 0)
    tables(0)
    forward(4, (9,), 1)
    forward(5, (10,), 1)
    for n in (3, 7, 8):
        for i in range(2):
            forward(n, (), i)
    tables(1)
    to_scalar.wait()

    places = []
    for rho in range(4):
        owner = 2 * ((h + rho // 2) % 2) + (c + rho % 2) % 2
        for i in range(2):
            places.append(2 * owner + i)
    group = lax.broadcasted_iota(jnp.int32, (4 * BLK, LANES), 1) // 16

    def ring(dd, kk):
        return pltpu.make_async_remote_copy(
            src_ref=sendbuf.at[dd, kk], dst_ref=recvbuf.at[dd, kk],
            send_sem=rs.at[dd, kk], recv_sem=rr.at[dd, kk],
            device_id=column(order(dd)), device_id_type=MESH,
        )

    def phonons_of(dd, kk):
        k = 8 * ((x + order(dd % 4)) % 4) + 2 * g + kk
        return [inv[k, place] for place in places]

    def prepare(dd, kk, half):
        for slot, q in enumerate(phonons_of(dd, kk)):
            if slot // 4 != half:
                continue
            s = shift[q] % 8
            early = tab[slot, s].astype(F32)
            late = tab[slot, 8 + s].astype(F32)
            mix = (emit[q] * early + absorb[q] * late).astype(BF16)
            for r in range(2):
                lanes = slice(r * LANES, (r + 1) * LANES)
                rhs[kk, slot % 4 * LANES : (slot % 4 + 1) * LANES, lanes] = mix[r, :LANES]
                ends[dd % 4, kk, slot * 16 : (slot + 1) * 16, lanes] = mix[r, LANES:]

    def project(dd, kk, half):
        phonons = phonons_of(dd, kk)
        lhs = jnp.concatenate([cmain[q] for q in phonons[4 * half : 4 * half + 4]], axis=1)
        part = jnp.dot(lhs, rhs[kk], preferred_element_type=F32)
        if half == 0:
            proj[dd, kk] = part
            return
        last = ctail[phonons[0]]
        for slot in range(1, 8):
            last = jnp.where(group == slot, ctail[phonons[slot]], last)
        part = part + jnp.dot(last, ends[dd, kk], preferred_element_type=F32)
        proj[dd, kk] = proj[dd, kk] + part

    def gather(dd, kk):
        for r in range(2):
            for m in range(0, BLK, 8):
                total = None
                for j in range(4):
                    piece = proj[dd, kk, j * BLK + m : j * BLK + m + 8, r * LANES : (r + 1) * LANES]
                    piece = jnp.take_along_axis(piece, lanes_from[j], axis=1, mode="promise_in_bounds")
                    total = piece if total is None else total + piece
                mine[kk, r, m : m + 8] = total
            sendbuf[dd, kk, r] = mine[kk, r].astype(BF16)

    prepare(0, 0, 0)

    @pl.loop(0, 4)
    def _(dd):
        prepare(dd, 1, 0)
        project(dd, 0, 0)
        table(2, dd // 2, dd % 2)
        prepare(dd + 1, 0, 0)
        project(dd, 1, 0)

    for n in (6, 9, 10):
        for i in range(2):
            forward(n, (), i)
    tables(3)
    prepare(0, 0, 1)
    prepare(0, 1, 1)
    project(0, 0, 1)
    gather(0, 0)
    project(0, 1, 1)
    prepare(1, 0, 1)
    ring(0, 0).start()
    gather(0, 1)
    prepare(1, 1, 1)
    project(1, 0, 1)
    prepare(2, 0, 1)
    project(1, 1, 1)
    ring(0, 1).start()

    @pl.loop(2, 4)
    def _(dd):
        gather(dd - 1, 0)
        gather(dd - 1, 1)
        prepare(dd, 1, 1)
        project(dd, 0, 1)
        prepare(dd + 1, 0, 1)
        project(dd, 1, 1)
        ring(dd - 1, 0).start()
        ring(dd - 1, 1).start()

    gather(3, 0)
    gather(3, 1)
    keep = pltpu.make_async_copy(mine, mine_out, lsem.at[1])
    keep.start()
    for pair in hops:
        for piece in pair:
            piece.wait_send()
    keep.wait()
    for dd in range(3):
        for kk in range(2):
            ring(dd, kk).wait_send()
            ring(dd, kk).wait_recv()


def on_device(green, coupling, kdiff, shift, emit_weight, absorb_weight, neighbours):
    hbm = pl.BlockSpec(memory_space=pl.ANY)
    block = (2, 2, BLK, LANES)
    total, parts = pl.pallas_call(
        kernel,
        out_shape=(jax.ShapeDtypeStruct(block, F32), jax.ShapeDtypeStruct((3,) + block, BF16)),
        in_specs=[hbm] * 7,
        out_specs=(hbm, hbm),
        scratch_shapes=[
            pltpu.VMEM(block, BF16),
            pltpu.VMEM((NK, 4 * BLK * BLK), BF16),
            pltpu.VMEM((NK, 4 * BLK, LANES), BF16),
            pltpu.VMEM((NK, 4 * BLK, LANES), BF16),
            pltpu.VMEM((FOLD, 512, LANES), F32),
            pltpu.VMEM((FOLD, 512, LANES), F32),
            pltpu.VMEM((4, 3) + block, BF16),
            pltpu.VMEM((8, 16, 2, BLK, LANES), BF16),
            pltpu.VMEM((2, 4 * LANES, 2 * LANES), BF16),
            pltpu.VMEM((4, 2, LANES, 2 * LANES), BF16),
            pltpu.VMEM(block, F32),
            pltpu.VMEM((4,) + block, BF16),
            pltpu.VMEM((4, 8, LANES), jnp.int32),
            pltpu.VMEM((4, 2, 4 * BLK, 2 * LANES), F32),
            pltpu.VMEM((NK, NK), jnp.int32),
            pltpu.VMEM((NK, LANES), jnp.int32),
            pltpu.SMEM((NK, LANES), jnp.int32),
            pltpu.SMEM((NK,), jnp.int32),
            pltpu.SMEM((NK,), F32),
            pltpu.SMEM((NK,), F32),
            pltpu.SMEM((4, NA), jnp.int32),
            pltpu.SemaphoreType.DMA((4,)),
            pltpu.SemaphoreType.DMA((6,)),
            pltpu.SemaphoreType.DMA((22,)),
            pltpu.SemaphoreType.DMA((22,)),
            pltpu.SemaphoreType.DMA((3, 2)),
            pltpu.SemaphoreType.DMA((3, 2)),
        ],
        compiler_params=pltpu.CompilerParams(
            collective_id=0, has_side_effects=True, vmem_limit_bytes=62 * 2**20
        ),
    )(green, coupling, kdiff, shift, emit_weight, absorb_weight, neighbours.T)
    return total + (parts[0].astype(F32) + parts[1].astype(F32) + parts[2].astype(F32))


def solution(mesh):
    return jax.shard_map(
        on_device,
        mesh=mesh,
        in_specs=(P("kz", None, None, "en"), P(), P(), P(), P(), P(), P()),
        out_specs=P("kz", None, None, "en"),
        check_vma=False,
    )
```

```python
import jax
import jax.numpy as jnp
from jax import lax
from jax.experimental import pallas as pl
from jax.experimental.pallas import tpu as pltpu
from jax.sharding import PartitionSpec as P

BLK = 144
LANES = 128
NA = 16
NK = 32
SPAN = 16 * BLK
FOLD = 6
MESH = pl.DeviceIdType.MESH
BF16 = jnp.bfloat16
F32 = jnp.float32


def relay_couple(cbuf, cmain, ctail, head, tail, spread, part):
    for f in range(FOLD):
        chunk = part * FOLD + f
        base = chunk * SPAN
        row = chunk * 16
        if not isinstance(part, int):
            base, row = pl.multiple_of(base, LANES), pl.multiple_of(row, 16)
        for half in range(NK // 16):
            x = cbuf[16 * half : 16 * half + 16, pl.ds(base, SPAN)]
            for m in range(16):
                o = m * BLK
                a = x[:, o : o + LANES].astype(F32)
                b = x[:, o + LANES : o + BLK].astype(F32)
                for u in range(2):
                    r0 = ((2 * half + u) * 16 + m) * 8
                    head[f, r0 : r0 + 8, :] = a[8 * u : 8 * u + 8]
                    tail[f, r0 : r0 + 8, 0:16] = b[8 * u : 8 * u + 8]
            tips = []
            for u in range(2):
                for v in range(8):
                    q = 16 * half + 8 * u + v
                    rows = pl.ds((2 * half + u) * 128 + v, 16, stride=8)
                    cmain[q, pl.ds(row, 16), :] = head[f, rows, :].astype(BF16)
                    tips.append(tail[f, rows, :].astype(BF16))
            wide = jnp.dot(jnp.concatenate(tips, 0), spread, preferred_element_type=F32)
            for v in range(16):
                ctail[16 * half + v, pl.ds(row, 16), :] = wide[16 * v : 16 * v + 16].astype(BF16)


def shift_tables(table, before, own, after):
    for s in range(1, 8):
        w = NA * s
        table[s] = jnp.concatenate([before[:, LANES - w :], own[:, : LANES - w]], 1)
        table[8 + s] = jnp.concatenate([own[:, w:], after[:, :w]], 1)
    table[0] = before
    table[8] = after


def invert(kd, first):
    lane = lax.broadcasted_iota(jnp.int32, (NK, NK), 1)
    wide = lax.broadcasted_iota(jnp.int32, (NK, LANES), 1)
    result = jnp.zeros((NK, LANES), jnp.int32)
    for i in range(8):
        q = jnp.sum(jnp.where(kd == first + i, lane, 0), axis=1, keepdims=True)
        result = jnp.where(wide == i, jnp.minimum(q, NK - 1), result)
    return result


def sources(nbr, j):
    lane = lax.broadcasted_iota(jnp.int32, (8, LANES), 1)
    atom = lane % NA
    source = lane - atom
    for a in range(NA):
        source = jnp.where(atom == a, source + nbr[j, a], source)
    return source


def kernel(
    green, couple, kdiff, shift_in, emit_in, absorb_in, nbr_in, mine_out, recvbuf,
    own, cbuf, cmain, ctail, head, tail, got, tab, rhs, ends, mine, sendbuf, lanes_from, proj,
    kd, invv, inv, shift, emit, absorb, nbr,
    csem, lsem, gs, gr, rs, rr,
):
    kz, en = lax.axis_index("kz"), lax.axis_index("en")
    count = lax.axis_size("en")
    x, g = kz // 4, kz % 4
    h, c = g // 2, g % 2
    partner = (kz + 1 - 2 * c, en)
    across = (kz + 2 - 4 * h, en)
    later = (kz, (en + 1) % count)
    earlier = (kz, (en + count - 1) % count)

    def order(dd):
        return (2 + 3 * dd + 3 * (dd // 2) + 2 * (dd // 3)) % 4

    def column(d):
        return ((kz + 4 * d) % 16, en)

    def fetch(j):
        cols = pl.ds(j * BLK * BLK, BLK * BLK)
        return pltpu.make_async_copy(couple.at[:, cols], cbuf.at[:, cols], csem.at[j])

    barrier = pltpu.get_barrier_semaphore()
    for peer in (partner, across, later, earlier, column(1), column(2), column(3)):
        pl.semaphore_signal(barrier, inc=1, device_id=peer, device_id_type=MESH)
    loads = [
        pltpu.make_async_copy(src, dst, lsem.at[n])
        for n, (src, dst) in enumerate(
            ((kdiff, kd), (shift_in, shift), (emit_in, emit), (absorb_in, absorb), (nbr_in, nbr), (green, own))
        )
    ]
    for load in loads:
        load.start()
    for j in range(4):
        fetch(j).start()
    tail[...] = jnp.zeros_like(tail)
    pl.semaphore_wait(barrier, 7)

    def hop(n, src, dst, peer):
        return [
            pltpu.make_async_remote_copy(
                src_ref=src.at[i], dst_ref=dst.at[i],
                send_sem=gs.at[2 * n + i], recv_sem=gr.at[2 * n + i],
                device_id=peer, device_id_type=MESH,
            )
            for i in range(2)
        ]

    hops = [
        hop(0, green, got.at[2, 1], across),
        hop(1, green, got.at[0, 0], later),
        hop(2, green, got.at[0, 2], earlier),
        hop(3, green, got.at[1, 1], partner),
        hop(4, got.at[2, 1], got.at[2, 0], later),
        hop(5, got.at[2, 1], got.at[2, 2], earlier),
        hop(6, got.at[2, 1], got.at[3, 1], partner),
        hop(7, got.at[0, 0], got.at[1, 0], partner),
        hop(8, got.at[0, 2], got.at[1, 2], partner),
        hop(9, got.at[2, 0], got.at[3, 0], partner),
        hop(10, got.at[2, 2], got.at[3, 2], partner),
    ]

    def forward(n, onward, i):
        hops[n][i].wait_recv()
        for target in onward:
            hops[target][i].start()

    for i in range(2):
        for n in range(4):
            hops[n][i].start()
    for load in loads:
        load.wait()
    invv[...] = invert(kd[...], 8 * x)
    to_scalar = pltpu.make_async_copy(invv, inv, lsem.at[0])
    to_scalar.start()
    for j in range(4):
        lanes_from[j] = sources(nbr, j)

    def table(rho, i, r):
        here = own[i, r] if rho == 0 else got[rho, 1, i, r]
        before, after = got[rho, 0, i, r], got[rho, 2, i, r]
        before = jnp.where(en > 0, before, jnp.zeros_like(before))
        after = jnp.where(en < count - 1, after, jnp.zeros_like(after))
        shift_tables(tab.at[2 * rho + i, :, r], before, here, after)

    def tables(rho):
        @pl.loop(0, 2)
        def _(i):
            for r in range(2):
                table(rho, i, r)

    fine = lax.broadcasted_iota(jnp.int32, (LANES, LANES), 1) % 16
    spread = jnp.where(lax.broadcasted_iota(jnp.int32, (LANES, LANES), 0) == fine, 1.0, 0.0).astype(BF16)

    @pl.loop(0, BLK * 4 // 16 // FOLD)
    def _(part):
        for j, at in enumerate((0, 0, 3, 4)):
            @pl.when(part == at)
            def _():
                fetch(j).wait()

        relay_couple(cbuf, cmain, ctail, head, tail, spread, part)

        @pl.when(part == 1)
        def _():
            forward(0, (4, 5, 6), 0)

        @pl.when(part == 2)
        def _():
            forward(1, (7,), 0)
            forward(2, (8,), 0)

        @pl.when(part == 3)
        def _():
            forward(0, (4, 5, 6), 1)
            forward(1, (7,), 1)
            forward(2, (8,), 1)

    forward(4, (9,), 0)
    forward(5, (10,), 0)
    tables(0)
    forward(4, (9,), 1)
    forward(5, (10,), 1)
    for n in (3, 7, 8):
        for i in range(2):
            forward(n, (), i)
    tables(1)
    to_scalar.wait()

    places = []
    for rho in range(4):
        owner = 2 * ((h + rho // 2) % 2) + (c + rho % 2) % 2
        for i in range(2):
            places.append(2 * owner + i)
    group = lax.broadcasted_iota(jnp.int32, (4 * BLK, LANES), 1) // 16

    def ring(dd, kk):
        return pltpu.make_async_remote_copy(
            src_ref=sendbuf.at[dd, kk], dst_ref=recvbuf.at[dd, kk],
            send_sem=rs.at[dd, kk], recv_sem=rr.at[dd, kk],
            device_id=column(order(dd)), device_id_type=MESH,
        )

    def phonons_of(dd, kk):
        k = 8 * ((x + order(dd % 4)) % 4) + 2 * g + kk
        return [inv[k, place] for place in places]

    def prepare(dd, kk, half):
        for slot, q in enumerate(phonons_of(dd, kk)):
            if slot // 4 != half:
                continue
            s = shift[q] % 8
            early = tab[slot, s].astype(F32)
            late = tab[slot, 8 + s].astype(F32)
            mix = (emit[q] * early + absorb[q] * late).astype(BF16)
            for r in range(2):
                lanes = slice(r * LANES, (r + 1) * LANES)
                rhs[kk, slot % 4 * LANES : (slot % 4 + 1) * LANES, lanes] = mix[r, :LANES]
                ends[dd % 4, kk, slot * 16 : (slot + 1) * 16, lanes] = mix[r, LANES:]

    def project(dd, kk, half):
        phonons = phonons_of(dd, kk)
        lhs = jnp.concatenate([cmain[q] for q in phonons[4 * half : 4 * half + 4]], axis=1)
        part = jnp.dot(lhs, rhs[kk], preferred_element_type=F32)
        if half == 0:
            proj[dd, kk] = part
            return
        last = ctail[phonons[0]]
        for slot in range(1, 8):
            last = jnp.where(group == slot, ctail[phonons[slot]], last)
        part = part + jnp.dot(last, ends[dd, kk], preferred_element_type=F32)
        proj[dd, kk] = proj[dd, kk] + part

    def gather(dd, kk):
        for r in range(2):
            for m in range(0, BLK, 8):
                total = None
                for j in range(4):
                    piece = proj[dd, kk, j * BLK + m : j * BLK + m + 8, r * LANES : (r + 1) * LANES]
                    piece = jnp.take_along_axis(piece, lanes_from[j], axis=1, mode="promise_in_bounds")
                    total = piece if total is None else total + piece
                mine[kk, r, m : m + 8] = total
            sendbuf[dd, kk, r] = mine[kk, r].astype(BF16)

    prepare(0, 0, 0)

    for rho in (2, 3):

        @pl.loop(2 * rho - 4, 2 * rho - 2)
        def _(dd):
            prepare(dd, 1, 0)
            project(dd, 0, 0)
            for r in range(2):
                table(rho, dd % 2, r)
            prepare(dd + 1, 0, 0)
            project(dd, 1, 0)

        if rho == 2:
            for n in (6, 9, 10):
                for i in range(2):
                    forward(n, (), i)

    prepare(0, 0, 1)
    prepare(0, 1, 1)
    project(0, 0, 1)
    gather(0, 0)
    project(0, 1, 1)
    prepare(1, 0, 1)
    ring(0, 0).start()
    gather(0, 1)
    prepare(1, 1, 1)
    project(1, 0, 1)
    prepare(2, 0, 1)
    project(1, 1, 1)
    ring(0, 1).start()

    @pl.loop(2, 4)
    def _(dd):
        gather(dd - 1, 0)
        gather(dd - 1, 1)
        prepare(dd, 1, 1)
        project(dd, 0, 1)
        prepare(dd + 1, 0, 1)
        project(dd, 1, 1)
        ring(dd - 1, 0).start()
        ring(dd - 1, 1).start()

    gather(3, 0)
    gather(3, 1)
    keep = pltpu.make_async_copy(mine, mine_out, lsem.at[1])
    keep.start()
    for pair in hops:
        for piece in pair:
            piece.wait_send()
    keep.wait()
    for dd in range(3):
        for kk in range(2):
            ring(dd, kk).wait_send()
            ring(dd, kk).wait_recv()


def on_device(green, coupling, kdiff, shift, emit_weight, absorb_weight, neighbours):
    hbm = pl.BlockSpec(memory_space=pl.ANY)
    block = (2, 2, BLK, LANES)
    total, parts = pl.pallas_call(
        kernel,
        out_shape=(jax.ShapeDtypeStruct(block, F32), jax.ShapeDtypeStruct((3,) + block, BF16)),
        in_specs=[hbm] * 7,
        out_specs=(hbm, hbm),
        scratch_shapes=[
            pltpu.VMEM(block, BF16),
            pltpu.VMEM((NK, 4 * BLK * BLK), BF16),
            pltpu.VMEM((NK, 4 * BLK, LANES), BF16),
            pltpu.VMEM((NK, 4 * BLK, LANES), BF16),
            pltpu.VMEM((FOLD, 512, LANES), F32),
            pltpu.VMEM((FOLD, 512, LANES), F32),
            pltpu.VMEM((4, 3) + block, BF16),
            pltpu.VMEM((8, 16, 2, BLK, LANES), BF16),
            pltpu.VMEM((2, 4 * LANES, 2 * LANES), BF16),
            pltpu.VMEM((4, 2, LANES, 2 * LANES), BF16),
            pltpu.VMEM(block, F32),
            pltpu.VMEM((4,) + block, BF16),
            pltpu.VMEM((4, 8, LANES), jnp.int32),
            pltpu.VMEM((4, 2, 4 * BLK, 2 * LANES), F32),
            pltpu.VMEM((NK, NK), jnp.int32),
            pltpu.VMEM((NK, LANES), jnp.int32),
            pltpu.SMEM((NK, LANES), jnp.int32),
            pltpu.SMEM((NK,), jnp.int32),
            pltpu.SMEM((NK,), F32),
            pltpu.SMEM((NK,), F32),
            pltpu.SMEM((4, NA), jnp.int32),
            pltpu.SemaphoreType.DMA((4,)),
            pltpu.SemaphoreType.DMA((6,)),
            pltpu.SemaphoreType.DMA((22,)),
            pltpu.SemaphoreType.DMA((22,)),
            pltpu.SemaphoreType.DMA((3, 2)),
            pltpu.SemaphoreType.DMA((3, 2)),
        ],
        compiler_params=pltpu.CompilerParams(
            collective_id=0, has_side_effects=True, vmem_limit_bytes=62 * 2**20
        ),
    )(green, coupling, kdiff, shift, emit_weight, absorb_weight, neighbours.T)
    return total + (parts[0].astype(F32) + parts[1].astype(F32) + parts[2].astype(F32))


def solution(mesh):
    return jax.shard_map(
        on_device,
        mesh=mesh,
        in_specs=(P("kz", None, None, "en"), P(), P(), P(), P(), P(), P()),
        out_specs=P("kz", None, None, "en"),
        check_vma=False,
    )
```
